32 devices in a mesh: row: 8 (over y, x, core), col: 4 (over z).
Axes of the slice: x: 2, y: 2, z: 4, core: 2. Of those that a mesh axis runs over, the one named last changes fastest.
Arguments:
- start_modes: float32 [32, 131072], P(None, ('row', 'col')), may hold values from -6 to 6
- energies: float32 [131072], P(('row', 'col')), may hold values from -0.5 to 0.5
- coupling: float32 [2048, 20, 4096], P('row', 'col'), may hold values from -0.078125 to 0.078125
- pattern: int32 [2048, 20], P('row', 'col'), may hold values from 0 to 2047, as said below
Outputs:
- filtered: float32 [32, 131072], P(None, ('row', 'col'))
- previous: float32 [32, 131072], P(None, ('row', 'col'))
The draws below stay inside these ranges and needn't reach their ends.
Inputs may be any that keep to these rules, and one draw needn't show every extreme that they name: In block row i, the 5 entries pattern[i, c * 5] to pattern[i, c * 5 + 4] are distinct block columns j with (j // 64) % 4 == c.
All inputs are finite; a program needn't handle non-finite values.
Results may differ from the reference program's by a relative error of at most 0.0001.
Values sent between devices are 32-bit elements; how exact they have to be, the bound alone decides.
A program may use at most 192 MiB of HBM per device.

```python
import jax
import jax.numpy as jnp
from jax import lax

BASIS = 131072
BLOCK = 64
SLOTS = 5
MODES = 32
DEGREE = 3
BLOCKS = 2048
COUPLED = 20
N_ROW = 8
N_COL = 4


def draw_pattern(key, part):
    block_count = BASIS // BLOCK
    group_size = block_count // N_COL
    per_piece = block_count // (N_ROW * N_COL)
    stride = group_size // SLOTS
    key_jitter, key_rotate = jax.random.split(key)
    jitter = jax.random.randint(key_jitter, (block_count, N_COL, SLOTS), 0, stride)
    rotate = jax.random.randint(key_rotate, (block_count, N_COL, 1), 0, group_size)
    offsets = (jnp.arange(SLOTS, dtype=jnp.int32)[None, None, :] * stride + jitter + rotate) % group_size
    piece_row = offsets // per_piece
    within = offsets % per_piece
    column = jnp.arange(N_COL, dtype=jnp.int32)[None, :, None]
    return ((piece_row * N_COL + column) * per_piece + within).reshape(block_count, N_COL * SLOTS).astype(jnp.int32)


def block_scale(key, shape, pieces, low, high):
    gain, own = 1.0, jax.random.fold_in(key, 6)
    for dim, parts in pieces:
        steps = jnp.exp(jax.random.uniform(jax.random.fold_in(own, dim), (parts,), jnp.float32, low / len(pieces), high / len(pieces)))
        gain = gain * jnp.repeat(steps, shape[dim] // parts).reshape([-1 if axis == dim else 1 for axis in range(len(shape))])
    return gain


def bell_draw(key, dims, deviation, reach, cuts=(), kind=jnp.bfloat16):
    values = jax.random.normal(key, dims, jnp.float32) * deviation
    if len(cuts) > 0:
        values = block_scale(key, dims, cuts, -0.22, 0.18) * values
    return jnp.clip(values, min=-reach, max=reach).astype(kind)


def setup_inputs(seed: int = 0) -> dict:
    keys = jax.random.split(jax.random.key(seed), 5)
    start_modes = bell_draw(keys[0], (MODES, BASIS), 1.0, 6.0, ((1, 32),), jnp.float32)
    energies = jnp.clip(jax.random.uniform(keys[1], (BASIS,), jnp.float32, -0.5, 0.5) * block_scale(keys[1], (BASIS,), ((0, 32),), -0.4, 0.0), -0.5, 0.5)
    coupling = bell_draw(keys[2], (BLOCKS, COUPLED, BLOCK * BLOCK), (4 * BLOCK * COUPLED) ** -0.5, 0.078125, ((0, 8), (1, 4)), jnp.float32)
    pattern = draw_pattern(jax.random.fold_in(keys[4], 71), 0)
    return {"start_modes": start_modes, "energies": energies, "coupling": coupling, "pattern": pattern}


def operate(vector, energies, coupling, pattern):
    mode_count = vector.shape[0]
    blocks = vector.reshape(mode_count, BLOCKS, BLOCK)
    group_rows = min(BLOCKS, 128)
    groups = BLOCKS // group_rows

    def block_rows(inputs):
        sub_mats, sub_cols = inputs
        picked = jnp.take(blocks, sub_cols.reshape(-1), axis=1).reshape(mode_count, group_rows, COUPLED, BLOCK)
        block_mats = sub_mats.reshape(group_rows, COUPLED, BLOCK, BLOCK)
        return jnp.einsum("mrsb,rsab->rma", picked, block_mats, precision=lax.Precision.HIGHEST)

    result = lax.map(block_rows, (coupling.reshape(groups, group_rows, COUPLED, BLOCK * BLOCK), pattern.reshape(groups, group_rows, COUPLED)))
    coupled = jnp.transpose(result, (2, 0, 1, 3)).reshape(mode_count, BASIS)
    return energies[None, :] * vector + coupled


def reference(start_modes, energies, coupling, pattern):
    previous = start_modes
    current = operate(start_modes, energies, coupling, pattern)
    for degree in range(DEGREE - 1):
        upcoming = 2.0 * operate(current, energies, coupling, pattern) - previous
        previous = current
        current = upcoming
    return current, previous
```

```python
import functools

import jax
import jax.numpy as jnp
from jax import lax
from jax.experimental import pallas as pl
from jax.experimental.pallas import tpu as pltpu
from jax.sharding import PartitionSpec as P

BLOCK = 64
DEGREE = 3
LANES = 128


def low_half(shape):
    return lax.broadcasted_iota(jnp.int32, shape, len(shape) - 1) < BLOCK


def split(x):
    high = x.astype(jnp.bfloat16)
    return high, (x - high.astype(jnp.float32)).astype(jnp.bfloat16)


def prepare_kernel(slots, c_ref, out_ref, stage):
    pairs = (slots + 1) // 2
    group = c_ref.shape[1]
    low = low_half((group, LANES))
    for k in range(pairs):
        for p in range(BLOCK // 2):
            first = c_ref[2 * k, :, p * LANES : (p + 1) * LANES]
            first_turned = pltpu.roll(first, BLOCK, 1)
            if 2 * k + 1 < slots:
                second = c_ref[2 * k + 1, :, p * LANES : (p + 1) * LANES]
                second_turned = pltpu.roll(second, BLOCK, 1)
            else:
                second = second_turned = jnp.zeros_like(first)
            stage[k, pl.ds(2 * p, group, stride=BLOCK), :] = jnp.where(low, first, second_turned)
            stage[k, pl.ds(2 * p + 1, group, stride=BLOCK), :] = jnp.where(low, first_turned, second)
    for k in range(pairs):
        for i in range(group):
            high, rest = split(stage[k, i * BLOCK : (i + 1) * BLOCK, :])
            out_ref[i, :BLOCK, k * LANES : (k + 1) * LANES] = high
            out_ref[i, BLOCK:, k * LANES : (k + 1) * LANES] = rest


def prepare(coupling):
    rows, slots, entries = coupling.shape
    group = 8
    pairs = (slots + 1) // 2
    return pl.pallas_call(
        functools.partial(prepare_kernel, slots),
        grid=(rows // group,),
        in_specs=[pl.BlockSpec((slots, group, entries), lambda g: (0, g, 0))],
        out_specs=pl.BlockSpec((group, 2 * BLOCK, pairs * LANES), lambda g: (g, 0, 0)),
        out_shape=jax.ShapeDtypeStruct((rows, 2 * BLOCK, pairs * LANES), jnp.bfloat16),
        scratch_shapes=[pltpu.VMEM((pairs, group * BLOCK, LANES), jnp.float32)],
        cost_estimate=pl.CostEstimate(flops=10 * coupling.size, bytes_accessed=9 * coupling.size, transcendentals=0),
        name="prepare",
    )(jnp.transpose(coupling, (1, 0, 2)))


def fill_blocks(gathered_ref, blocks, pieces, modes, tiles):
    low = low_half((modes, LANES))

    def piece(index, carry):
        for t in range(tiles):
            x = gathered_ref[index, :, t * LANES : (t + 1) * LANES]
            turned = pltpu.roll(x, BLOCK, 1)
            for side, value in enumerate((jnp.where(low, x, turned), jnp.where(low, turned, x))):
                high, rest = split(value)
                place = index * (2 * tiles) + 2 * t + side
                blocks[place, :modes, :] = high
                blocks[place, modes:, :] = rest
        return carry

    lax.fori_loop(0, pieces, piece, 0)


def couple_kernel(slots, places_ref, gathered_ref, c_ref, out_ref, blocks):
    step = pl.program_id(0)
    group = c_ref.shape[0]
    pieces, modes, piece_len = gathered_ref.shape

    @pl.when(step == 0)
    def _():
        fill_blocks(gathered_ref, blocks, pieces, modes, piece_len // LANES)

    low = low_half((2 * modes, LANES))
    low_out = low_half((modes, LANES))
    done = []
    for i in range(group):
        base = (step * group + i) * slots
        picked = [blocks[places_ref[base + s]] for s in range(slots)]
        sides = [
            jnp.where(low, picked[2 * k], picked[2 * k + 1]) if 2 * k + 1 < slots else picked[2 * k]
            for k in range((slots + 1) // 2)
        ]
        product = lax.dot_general(
            jnp.concatenate(sides, axis=1), c_ref[i], (((1,), (1,)), ((), ())), preferred_element_type=jnp.float32
        )
        total = product[:modes] + product[modes:]
        done.append(total + pltpu.roll(total, BLOCK, 1))
        if i % 2 == 1:
            out_ref[0, :, (i // 2) * LANES : (i // 2 + 1) * LANES] = jnp.where(low_out, done[i - 1], done[i])


def couple(gathered, places, prepared, slots, col_count):
    pieces, modes, piece_len = gathered.shape
    rows = prepared.shape[0]
    per_piece = piece_len // BLOCK
    group = min(16, per_piece)
    per_part = per_piece // group
    return pl.pallas_call(
        functools.partial(couple_kernel, slots),
        grid_spec=pltpu.PrefetchScalarGridSpec(
            num_scalar_prefetch=1,
            grid=(rows // group,),
            in_specs=[
                pl.BlockSpec(gathered.shape, lambda g, *_: (0, 0, 0), pipeline_mode=pl.Buffered(1)),
                pl.BlockSpec((group,) + prepared.shape[1:], lambda g, *_: (g, 0, 0)),
            ],
            out_specs=pl.BlockSpec((1, modes, group * BLOCK), lambda g, *_: (g // per_part, 0, g % per_part)),
            scratch_shapes=[pltpu.VMEM((pieces * per_piece, 2 * modes, LANES), jnp.bfloat16)],
        ),
        out_shape=jax.ShapeDtypeStruct((col_count, modes, piece_len), jnp.float32),
        cost_estimate=pl.CostEstimate(
            flops=4 * modes * prepared.size, bytes_accessed=2 * prepared.size + 8 * gathered.size, transcendentals=0
        ),
        name="couple",
    )(places, gathered, prepared)


def shards(start_modes, energies, coupling, pattern):
    col_count = lax.axis_size("col")
    piece_len = start_modes.shape[1]
    per_piece = piece_len // BLOCK
    slots = pattern.shape[1]
    places = (pattern // per_piece // col_count * per_piece + pattern % per_piece).reshape(-1)
    prepared = prepare(coupling)

    def operate(vector):
        gathered = lax.all_gather(vector, "row", axis=0, tiled=False)
        shares = couple(gathered, places, prepared, slots, col_count)
        share = lax.psum_scatter(shares, "col", scatter_dimension=0, tiled=True)[0]
        return energies[None, :] * vector + share

    previous = start_modes
    current = operate(start_modes)
    for degree in range(DEGREE - 1):
        upcoming = 2.0 * operate(current) - previous
        previous = current
        current = upcoming
    return (current, previous)


def solution(mesh):
    in_specs = (P(None, ("row", "col")), P(("row", "col")), P("row", "col", None), P("row", "col"))
    out_specs = (P(None, ("row", "col")), P(None, ("row", "col")))
    return jax.shard_map(shards, mesh=mesh, in_specs=in_specs, out_specs=out_specs, check_vma=False)
```

```python
import functools

import jax
import jax.numpy as jnp
from jax import lax
from jax.experimental import pallas as pl
from jax.experimental.pallas import tpu as pltpu
from jax.sharding import PartitionSpec as P

BLOCK = 64
DEGREE = 3
LANES = 128


def low_half(shape):
    return lax.broadcasted_iota(jnp.int32, shape, len(shape) - 1) < BLOCK


def split(x):
    high = x.astype(jnp.bfloat16)
    return high, (x - high.astype(jnp.float32)).astype(jnp.bfloat16)


MESH = pl.DeviceIdType.MESH


def filter_kernel(
    slots, n_row, n_col, halves,
    places_ref, start_ref, energies_ref, coupling_ref, filtered_ref, previous_ref,
    c_buf, stage, prepared, gathered, blocks, first_ref, partial, landed,
    c_sem, gather_send, gather_recv, share_send, share_recv,
):
    row, col = lax.axis_index("row"), lax.axis_index("col")
    chips = n_row // 2
    chip, core = row // 2, row % 2
    partner = chip * 2 + (1 - core)
    modes, piece_len = start_ref.shape
    part = modes // halves
    tiles = piece_len // LANES
    per_piece = piece_len // BLOCK
    rows = prepared.shape[0]
    group = min(16, per_piece)
    terms = (start_ref, first_ref, previous_ref, filtered_ref)

    def same_core(d):
        return (chip + d) % chips * 2 + core

    def other_core(d):
        return (chip + d) % chips * 2 + (1 - core)

    def share_of(k, h):
        return terms[k].at[pl.ds(h * part, part), :]

    barrier = pltpu.get_barrier_semaphore()
    for d in range(1, chips):
        pl.semaphore_signal(barrier, inc=1, device_id=(same_core(d), col), device_id_type=MESH)
    pl.semaphore_signal(barrier, inc=1, device_id=(partner, col), device_id_type=MESH)
    for d in range(1, n_col):
        pl.semaphore_signal(barrier, inc=1, device_id=(row, (col + d) % n_col), device_id_type=MESH)
    pl.semaphore_wait(barrier, chips + n_col - 1)

    def gather_copy(k, h, source, slot, sem, target):
        return pltpu.make_async_remote_copy(
            src_ref=source,
            dst_ref=gathered.at[k, h, slot],
            send_sem=gather_send.at[k, h, sem],
            recv_sem=gather_recv.at[k, h, slot],
            device_id=(target, col),
            device_id_type=MESH,
        )

    def own_copies(k, h):
        source = share_of(k, h)
        return [gather_copy(k, h, source, row, d, same_core(d)) for d in range(1, chips)] + [
            gather_copy(k, h, source, row, 0, partner)
        ]

    def passed_copies(k, h):
        return [
            gather_copy(k, h, gathered.at[k, h, same_core(-d)], same_core(-d), chips + d, partner)
            for d in range(1, chips)
        ]

    def arrival(k, h, slot):
        return gather_copy(k, h, gathered.at[k, h, slot], slot, 0, partner)

    def gather_start(k, h):
        for copy in own_copies(k, h):
            copy.start()
        gathered[k, h, row] = share_of(k, h)[...]

    def gather_finish(k, h):
        for d, copy in enumerate(passed_copies(k, h), 1):
            arrival(k, h, same_core(-d)).wait_recv()
            copy.start()
        arrival(k, h, partner).wait_recv()
        for d in range(1, chips):
            arrival(k, h, other_core(-d)).wait_recv()

    def share_copy(k, h, target):
        return pltpu.make_async_remote_copy(
            src_ref=partial.at[k, h, target],
            dst_ref=landed.at[k, h, col],
            send_sem=share_send.at[k, h, target],
            recv_sem=share_recv.at[k, h, col],
            device_id=(row, target),
            device_id_type=MESH,
        )

    def share_arrival(k, h, origin):
        return pltpu.make_async_remote_copy(
            src_ref=partial.at[k, h, origin],
            dst_ref=landed.at[k, h, origin],
            send_sem=share_send.at[k, h, origin],
            recv_sem=share_recv.at[k, h, origin],
            device_id=(row, origin),
            device_id_type=MESH,
        )

    def compute(k, h):
        low = low_half((part, LANES))
        low_picked = low_half((2 * part, LANES))

        def fill(index, carry):
            for t in range(tiles):
                x = gathered[k, h, index, :, t * LANES : (t + 1) * LANES]
                turned = pltpu.roll(x, BLOCK, 1)
                for side, value in enumerate((jnp.where(low, x, turned), jnp.where(low, turned, x))):
                    high, rest = split(value)
                    place = index * (2 * tiles) + 2 * t + side
                    blocks[place, :part, :] = high
                    blocks[place, part:, :] = rest
            return carry

        lax.fori_loop(0, n_row, fill, 0)

        def one_part(d, carry):
            target = (col + d) % n_col

            def some_rows(step, carry):
                first = target * per_piece + step * group
                done = []
                for i in range(group):
                    base = (first + i) * slots
                    picked = [blocks[places_ref[base + s]] for s in range(slots)]
                    sides = [
                        jnp.where(low_picked, picked[2 * q], picked[2 * q + 1]) if 2 * q + 1 < slots else picked[2 * q]
                        for q in range((slots + 1) // 2)
                    ]
                    product = lax.dot_general(
                        jnp.concatenate(sides, axis=1),
                        prepared[first + i],
                        (((1,), (1,)), ((), ())),
                        preferred_element_type=jnp.float32,
                    )
                    total = product[:part] + product[part:]
                    done.append(total + pltpu.roll(total, BLOCK, 1))
                width = group * BLOCK
                wide = [jnp.where(low, done[2 * q], done[2 * q + 1]) for q in range(group // 2)]
                partial[k, h, target, :, pl.ds(pl.multiple_of(step * width, width), width)] = jnp.concatenate(wide, axis=1)
                return carry

            lax.fori_loop(0, per_piece // group, some_rows, 0)
            return carry

        def one_sent(d, carry):
            one_part(d, carry)
            share_copy(k, h, (col + d) % n_col).start()
            return carry

        lax.fori_loop(1, n_col, one_sent, 0)
        one_part(0, 0)

    def update(k, h):
        for d in range(1, n_col):
            share_arrival(k, h, (col + d) % n_col).wait_recv()
        here = slice(h * part, (h + 1) * part)

        def tile(t, carry):
            at = pl.ds(pl.multiple_of(t * LANES, LANES), LANES)
            total = partial[k, h, col, :, at]
            for d in range(1, n_col):
                total = total + landed[k, h, (col + d) % n_col, :, at]
            total = energies_ref[:, at] * terms[k][here, at] + total
            if k > 0:
                total = 2.0 * total - terms[k - 1][here, at]
            terms[k + 1][here, at] = total
            return carry

        lax.fori_loop(0, tiles, tile, 0)

    for h in range(halves):
        gather_start(0, h)

    chunk = c_buf.shape[2]
    chunks = rows // chunk

    def fetch(index, slot):
        return pltpu.make_async_copy(
            coupling_ref.at[:, pl.ds(pl.multiple_of(index * chunk, chunk), chunk), :], c_buf.at[slot], c_sem.at[slot]
        )

    fetch(0, 0).start()

    def prepare_chunk(index, carry):
        slot = index % 2

        @pl.when(index + 1 < chunks)
        def _():
            fetch(index + 1, 1 - slot).start()

        fetch(index, slot).wait()
        pairs = (slots + 1) // 2
        low = low_half((chunk, LANES))
        for q in range(pairs):
            for p in range(BLOCK // 2):
                lane = slice(p * LANES, (p + 1) * LANES)
                one = c_buf[slot, 2 * q, :, lane]
                one_turned = pltpu.roll(one, BLOCK, 1)
                if 2 * q + 1 < slots:
                    two = c_buf[slot, 2 * q + 1, :, lane]
                    two_turned = pltpu.roll(two, BLOCK, 1)
                else:
                    two = two_turned = jnp.zeros_like(one)
                stage[q, pl.ds(2 * p, chunk, stride=BLOCK), :] = jnp.where(low, one, two_turned)
                stage[q, pl.ds(2 * p + 1, chunk, stride=BLOCK), :] = jnp.where(low, one_turned, two)
        for q in range(pairs):
            for i in range(chunk):
                high, rest = split(stage[q, i * BLOCK : (i + 1) * BLOCK, :])
                prepared[index * chunk + i, :BLOCK, q * LANES : (q + 1) * LANES] = high
                prepared[index * chunk + i, BLOCK:, q * LANES : (q + 1) * LANES] = rest
        return carry

    lax.fori_loop(0, chunks, prepare_chunk, 0)

    for k in range(DEGREE):
        for h in range(halves):
            if k > 0:
                update(k - 1, h)
                gather_start(k, h)
            gather_finish(k, h)
            compute(k, h)
    for h in range(halves):
        update(DEGREE - 1, h)
    for k in range(DEGREE):
        for h in range(halves):
            for copy in own_copies(k, h) + passed_copies(k, h):
                copy.wait_send()
            for d in range(1, n_col):
                share_copy(k, h, (col + d) % n_col).wait_send()


def shards(start_modes, energies, coupling, pattern):
    n_row, n_col = lax.axis_size("row"), lax.axis_size("col")
    modes, piece_len = start_modes.shape
    per_piece = piece_len // BLOCK
    rows, slots, entries = coupling.shape
    pairs = (slots + 1) // 2
    chunk, halves = 8, 2
    part = modes // halves
    places = (pattern // per_piece // n_col * per_piece + pattern % per_piece).reshape(-1)
    vmem = pl.BlockSpec(memory_space=pltpu.VMEM)
    filtered, previous = pl.pallas_call(
        functools.partial(filter_kernel, slots, n_row, n_col, halves),
        in_specs=[pl.BlockSpec(memory_space=pltpu.SMEM), vmem, vmem, pl.BlockSpec(memory_space=pl.ANY)],
        out_specs=[vmem, vmem],
        out_shape=[jax.ShapeDtypeStruct(start_modes.shape, jnp.float32)] * 2,
        scratch_shapes=[
            pltpu.VMEM((2, slots, chunk, entries), jnp.float32),
            pltpu.VMEM((pairs, chunk * BLOCK, LANES), jnp.float32),
            pltpu.VMEM((rows, 2 * BLOCK, pairs * LANES), jnp.bfloat16),
            pltpu.VMEM((DEGREE, halves, n_row, part, piece_len), jnp.float32),
            pltpu.VMEM((n_row * per_piece, 2 * part, LANES), jnp.bfloat16),
            pltpu.VMEM((modes, piece_len), jnp.float32),
            pltpu.VMEM((DEGREE, halves, n_col, part, piece_len), jnp.float32),
            pltpu.VMEM((DEGREE, halves, n_col, part, piece_len), jnp.float32),
            pltpu.SemaphoreType.DMA((2,)),
            pltpu.SemaphoreType.DMA((DEGREE, halves, n_row)),
            pltpu.SemaphoreType.DMA((DEGREE, halves, n_row)),
            pltpu.SemaphoreType.DMA((DEGREE, halves, n_col)),
            pltpu.SemaphoreType.DMA((DEGREE, halves, n_col)),
        ],
        compiler_params=pltpu.CompilerParams(collective_id=0, has_side_effects=True, vmem_limit_bytes=67043328),
        name="filter",
    )(places, start_modes, energies.reshape(1, -1), jnp.transpose(coupling, (1, 0, 2)))
    return filtered, previous


def solution(mesh):
    in_specs = (P(None, ("row", "col")), P(("row", "col")), P("row", "col", None), P("row", "col"))
    out_specs = (P(None, ("row", "col")), P(None, ("row", "col")))
    return jax.shard_map(shards, mesh=mesh, in_specs=in_specs, out_specs=out_specs, check_vma=False)
```
